32 devices in a mesh: pts: 16 (over z, x, core), cen: 2 (over y).
Axes of the slice: x: 2, y: 2, z: 4, core: 2. Of those that a mesh axis runs over, the one named last changes fastest.
Arguments:
- states: bfloat16 [8192, 512], P(('pts', 'cen')), may hold values from -48 to 48
- first_weight: bfloat16 [512, 1024], replicated, may hold values from -0.25 to 0.25
- first_bias: float32 [1024], replicated, may hold values from -4 to 4
- second_weight: bfloat16 [1024, 256], replicated, may hold values from -0.1875 to 0.1875
- centroids: bfloat16 [2, 4096, 256], P('cen'), may hold values from -3.59375 to 3.59375
Outputs:
- new_centroids: float32 [2, 4096, 256], P('cen', 'pts')
- sample_blended_penalty: float32 [8192], P(('pts', 'cen'))
The draws below stay inside these ranges and needn't reach their ends.
All inputs are finite; a program needn't handle non-finite values.
Results may differ from the reference program's by a relative error of at most 0.0061.
Values may be sent and summed in bfloat16 or wider, within the bound.
A program may use at most 128 MiB of HBM per device.

```python
import math
import jax
import jax.numpy as jnp
from jax import lax

SD = 512
HID = 1024
E = 256
K_DEV = 4096
NPTS = 8192
N_CEN = 2


def draw_states(key, part):
    first_key = jax.random.fold_in(jax.random.fold_in(key, 11), 0)
    base = jnp.clip(jax.random.normal(first_key, (NPTS, SD), jnp.float32), -6.0, 6.0)
    return base.astype(jnp.bfloat16)


def levels(key, shape, cuts, smallest, high):
    def one(position, parts):
        heights = jax.random.uniform(jax.random.fold_in(jax.random.fold_in(key, 6), position), (parts,), jnp.float32, smallest / len(cuts), high / len(cuts))
        return jnp.repeat(jnp.exp(heights), shape[position] // parts).reshape((-1,) + (1,) * (len(shape) - position - 1))

    gain = one(*cuts[0])
    for cut in cuts[1:]:
        gain = gain * one(*cut)
    return gain


def bell_draw(own_key, dims, width, limit, pieces=(), held_as=jnp.bfloat16):
    result = width * jax.random.normal(own_key, dims, jnp.float32)
    if pieces:
        result = result * levels(own_key, dims, pieces, -0.22, 0.18)
    return jnp.clip(result, -limit, limit).astype(held_as)


def setup_inputs(seed: int = 0) -> dict:
    arg_keys = jax.random.split(jax.random.key(seed), 6)
    states = draw_states(jax.random.fold_in(arg_keys[5], 71), 0)
    first_weight = bell_draw(arg_keys[1], (SD, HID), SD ** -0.5, 0.25)
    first_bias = bell_draw(arg_keys[2], (HID,), 1.0, 4.0, (), jnp.float32)
    second_weight = bell_draw(arg_keys[3], (HID, E), HID ** -0.5, 0.1875)
    centroids = bell_draw(arg_keys[4], (N_CEN, K_DEV, E), 0.6, 3.59375, ((0, 2),))
    return {"states": states, "first_weight": first_weight, "first_bias": first_bias, "second_weight": second_weight, "centroids": centroids}


smoothing_scale = 16.0


def encode(states, first_weight, first_bias, second_weight):
    pre = jnp.dot(states, first_weight, preferred_element_type=jnp.float32) + first_bias
    hidden = jax.nn.gelu(pre).astype(jnp.bfloat16)
    return jnp.dot(hidden, second_weight, preferred_element_type=jnp.float32).astype(jnp.bfloat16)


def scores_of(rows, centers):
    inner_pairing_matrix = lax.dot_general(rows, centers, (((1,), (1,)), ((), ())), preferred_element_type=jnp.float32)
    sample_length_squared = jnp.sum(jnp.square(rows.astype(jnp.float32)), axis=1)
    center_length_squared = jnp.sum(jnp.square(centers.astype(jnp.float32)), axis=1)
    return (2.0 * inner_pairing_matrix - center_length_squared[None, :] - sample_length_squared[:, None]) / smoothing_scale


def reference(states, first_weight, first_bias, second_weight, centroids):
    codes = encode(states, first_weight, first_bias, second_weight)
    embedding_dimension = codes.shape[1]
    centers = centroids.reshape(-1, embedding_dimension)
    total_rows = codes.shape[0]
    row_block = math.gcd(total_rows, 1024)

    def row_stats(block):
        scores = scores_of(block, centers)
        running_maximum = jnp.max(scores, axis=1)
        running_sum = jnp.sum(jnp.exp(scores - running_maximum[:, None]), axis=1)
        return running_maximum, running_sum

    tracked_peaks, tracked_totals = lax.map(row_stats, codes.reshape(total_rows // row_block, row_block, embedding_dimension))
    tracked_peaks = tracked_peaks.reshape(-1)
    tracked_totals = tracked_totals.reshape(-1)
    sample_blended_penalty = -(smoothing_scale / embedding_dimension) * (tracked_peaks + jnp.log(tracked_totals))
    count_centers = centers.shape[0]
    center_block = math.gcd(count_centers, 1024)

    def center_sums(group):
        scores = scores_of(codes, group)
        resp = jnp.exp(scores - tracked_peaks[:, None]) / tracked_totals[:, None]
        counts = jnp.sum(resp, axis=0)
        weighted = lax.dot_general(resp.astype(jnp.bfloat16), codes, (((0,), (0,)), ((), ())), preferred_element_type=jnp.float32)
        return weighted, counts

    weighted, counts = lax.map(center_sums, centers.reshape(count_centers // center_block, center_block, embedding_dimension))
    weighted = weighted.reshape(count_centers, embedding_dimension)
    counts = counts.reshape(count_centers)
    fresh = (weighted + centers.astype(jnp.float32)) / (counts + 1.0)[:, None]
    return fresh.reshape(centroids.shape), sample_blended_penalty
```

```python
import functools

import jax
import jax.numpy as jnp
from jax import lax
from jax.experimental import pallas as pl
from jax.experimental.pallas import tpu as pltpu
from jax.sharding import PartitionSpec as P

smoothing_scale = 16.0
MESH = pl.DeviceIdType.MESH
NT = (((1,), (1,)), ((), ()))


def encode(states, first_weight, first_bias, second_weight):
    pre = jnp.dot(states, first_weight, preferred_element_type=jnp.float32) + first_bias
    hidden = jax.nn.gelu(pre).astype(jnp.bfloat16)
    return jnp.dot(hidden, second_weight, preferred_element_type=jnp.float32).astype(jnp.bfloat16)


def scaled_squares(rows):
    wide = rows.astype(jnp.float32)
    return jnp.sum(wide * wide, axis=1, keepdims=True) / smoothing_scale


def kernel(
    n_pts, n_cen, codes_ref, cen_ref, out_ref, pen_ref,
    allc, stat, norm, weighted, counts, own_sq,
    recv, half, stat_recv, norm_recv,
    send_z, send_x, send_c, send_core, send_hx, send_hc, send_stat, send_norm, own_sem,
):
    n, width = codes_ref.shape
    n_z = n_pts // 4
    p, c = lax.axis_index("pts"), lax.axis_index("cen")
    core, x, z = lax.rem(p, 2), lax.rem(p // 2, 2), p // 4

    def pts_of(zi, xi, ki):
        return (zi * 2 + xi) * 2 + ki

    def z_at(k):
        return lax.rem(z + k, n_z)

    def c_at(j):
        return lax.rem(c + j, n_cen)

    def block(zi, xi, ki, ci):
        return pts_of(zi, xi, ki) * n_cen + ci

    x_peer = (pts_of(z, 1 - x, core), c)
    core_peer = (pts_of(z, x, 1 - core), c)
    mine = block(z, x, core, c)

    def remote(src, dst, send_sem, recv_sem, peer):
        return pltpu.make_async_remote_copy(
            src_ref=src, dst_ref=dst, send_sem=send_sem, recv_sem=recv_sem,
            device_id=peer, device_id_type=MESH,
        )

    sent = []

    def push(copy):
        copy.start()
        sent.append(copy)

    def whole(b, send_sem, peer, src=None):
        push(remote(allc.at[b] if src is None else src, allc.at[b], send_sem, recv.at[b], peer))

    def part(b, h, send_sem, peer):
        rows = pl.ds(h * (n // 2), n // 2)
        push(remote(allc.at[b, rows], allc.at[b, rows], send_sem, half.at[b, h], peer))

    def arrived(b):
        remote(allc.at[b], allc.at[b], own_sem, recv.at[b], core_peer).wait_recv()

    def part_arrived(b, h):
        rows = pl.ds(h * (n // 2), n // 2)
        remote(allc.at[b, rows], allc.at[b, rows], own_sem, half.at[b, h], core_peer).wait_recv()

    barrier = pltpu.get_barrier_semaphore()
    for k in range(1, n_pts):
        pl.semaphore_signal(
            barrier, inc=1, device_id=(lax.rem(p + k, n_pts), c), device_id_type=MESH
        )
    for j in range(1, n_cen):
        pl.semaphore_signal(barrier, inc=1, device_id=(p, c_at(j)), device_id_type=MESH)
    pl.semaphore_wait(barrier, n_pts - 1 + n_cen - 1)

    own = pltpu.make_async_copy(codes_ref, allc.at[mine], own_sem)
    own.start()
    for j in range(1, n_cen):
        whole(mine, send_c.at[0, j], (p, c_at(j)), codes_ref)
    for k in range(1, n_z):
        whole(mine, send_z.at[k], (pts_of(z_at(k), x, core), c), codes_ref)
    whole(mine, send_x.at[0], x_peer, codes_ref)
    whole(mine, send_core.at[0, 0, 0], core_peer, codes_ref)
    own.wait()

    owned = out_ref.shape[0]
    own_rows = pl.ds(pl.multiple_of(p * owned, owned), owned)
    own_sq[...] = scaled_squares(cen_ref[0, own_rows, :])

    for k in range(1, n_z):
        b = block(z_at(k), x, core, c)
        arrived(b)
        whole(b, send_x.at[k], x_peer)
        for j in range(1, n_cen):
            whole(b, send_c.at[k, j], (p, c_at(j)))
        whole(b, send_core.at[k, 0, 0], core_peer)

    def from_cen(k):
        for j in range(1, n_cen):
            b = block(z_at(k), x, core, c_at(j))
            arrived(b)
            part(b, 1, send_hx.at[k, j], x_peer)
            whole(b, send_core.at[k, 0, j], core_peer)

    from_cen(0)

    tile = min(256, cen_ref.shape[1])
    group_rows = n * n_cen
    group = pl.ds(p * n_cen, n_cen)

    def stats_step(i, carry):
        peak, total = carry
        centers = cen_ref[0, pl.ds(pl.multiple_of(i * tile, tile), tile), :]
        rows = allc[group].reshape(group_rows, width)
        scores = lax.dot_general(centers, rows, NT, preferred_element_type=jnp.float32)
        scores = scores * (2.0 / smoothing_scale) - scaled_squares(centers)
        peak_next = jnp.maximum(peak, jnp.max(scores, axis=0, keepdims=True))
        total_next = total * jnp.exp(peak - peak_next) + jnp.sum(
            jnp.exp(scores - peak_next), axis=0, keepdims=True
        )
        return peak_next, total_next

    peak, total = lax.fori_loop(
        0,
        cen_ref.shape[1] // tile,
        stats_step,
        (
            jnp.full((1, group_rows), -jnp.inf, jnp.float32),
            jnp.zeros((1, group_rows), jnp.float32),
        ),
    )
    first = lax.broadcasted_iota(jnp.int32, (8, n), 0) == 0
    for j in range(n_cen):
        cols = slice(j * n, (j + 1) * n)
        stat[c, j] = jnp.where(first, peak[:, cols], total[:, cols])
    for j in range(1, n_cen):
        push(remote(stat.at[c], stat.at[c], send_stat.at[j], stat_recv.at[c], (p, c_at(j))))

    for k in range(n_z):
        b = block(z_at(k), 1 - x, core, c)
        arrived(b)
        for j in range(1, n_cen):
            part(b, 0, send_hc.at[k, j], (p, c_at(j)))
        whole(b, send_core.at[k, 1, 0], core_peer)
        if k > 0:
            from_cen(k)

    for j in range(1, n_cen):
        s = c_at(j)
        remote(stat.at[s], stat.at[s], own_sem, stat_recv.at[s], (p, s)).wait_recv()
    for j in range(n_cen):
        top = stat[0, j][0:1, :]
        for s in range(1, n_cen):
            top = jnp.maximum(top, stat[s, j][0:1, :])
        mass = jnp.zeros_like(top)
        for s in range(n_cen):
            piece = stat[s, j]
            mass = mass + piece[1:2, :] * jnp.exp(piece[0:1, :] - top)
        norm[p, j] = jnp.broadcast_to(top + jnp.log(mass), (8, n))
    for k in range(1, n_pts):
        push(
            remote(
                norm.at[p], norm.at[p], send_norm.at[k], norm_recv.at[p],
                (lax.rem(p + k, n_pts), c),
            )
        )
    wide = codes_ref[...].astype(jnp.float32)
    lengths = lax.dot_general(
        jnp.ones((8, width), jnp.float32), wide * wide, NT,
        preferred_element_type=jnp.float32, precision=lax.Precision.HIGHEST,
    )
    pen_ref[...] = (-(smoothing_scale / width)) * (
        norm[p, c][0:1, :] - lengths[0:1, :] / smoothing_scale
    )

    for k in range(n_z):
        for j in range(1, n_cen):
            b = block(z_at(k), 1 - x, core, c_at(j))
            part_arrived(b, 0)
            part_arrived(b, 1)
            whole(b, send_core.at[k, 1, j], core_peer)

    for k in range(1, n_pts):
        s = lax.rem(p + k, n_pts)
        remote(norm.at[s], norm.at[s], own_sem, norm_recv.at[s], (s, c)).wait_recv()

    weighted[...] = jnp.zeros_like(weighted)
    counts[...] = jnp.zeros_like(counts)

    def consume(zi, xi, ki, ci):
        rows = allc[block(zi, xi, ki, ci)]
        scores = lax.dot_general(
            cen_ref[0, own_rows, :], rows, NT, preferred_element_type=jnp.float32
        )
        shift = norm[pts_of(zi, xi, ki), ci][0:1, :]
        resp = jnp.exp(scores * (2.0 / smoothing_scale) - own_sq[...] - shift)
        lanes = resp[:, 0:128]
        for q in range(1, n // 128):
            lanes = lanes + resp[:, q * 128:(q + 1) * 128]
        counts[...] += lanes
        weighted[...] += jnp.dot(
            resp.astype(jnp.bfloat16), rows, preferred_element_type=jnp.float32
        )

    def same_core(i, _):
        consume(i // (2 * n_cen), lax.rem(i // n_cen, 2), core, lax.rem(i, n_cen))
        return 0

    def other_core(i, _):
        zi, xi, ci = i // (2 * n_cen), lax.rem(i // n_cen, 2), lax.rem(i, n_cen)
        arrived(block(zi, xi, 1 - core, ci))
        consume(zi, xi, 1 - core, ci)
        return 0

    lax.fori_loop(0, n_z * 2 * n_cen, same_core, 0)
    lax.fori_loop(0, n_z * 2 * n_cen, other_core, 0)

    tally = jnp.sum(counts[...], axis=1, keepdims=True)
    out_ref[...] = (weighted[...] + cen_ref[0, own_rows, :].astype(jnp.float32)) / (tally + 1.0)
    for copy in sent:
        copy.wait_send()


def body(n_pts, n_cen, states, first_weight, first_bias, second_weight, centroids):
    codes = encode(states, first_weight, first_bias, second_weight)
    n, width = codes.shape
    owned = centroids.shape[1] // n_pts
    n_z = n_pts // 4
    dma = pltpu.SemaphoreType.DMA
    fresh, penalty = pl.pallas_call(
        functools.partial(kernel, n_pts, n_cen),
        out_shape=(
            jax.ShapeDtypeStruct((owned, width), jnp.float32),
            jax.ShapeDtypeStruct((1, n), jnp.float32),
        ),
        in_specs=[pl.BlockSpec(memory_space=pltpu.VMEM)] * 2,
        out_specs=(pl.BlockSpec(memory_space=pltpu.VMEM),) * 2,
        scratch_shapes=[
            pltpu.VMEM((n_pts * n_cen, n, width), jnp.bfloat16),
            pltpu.VMEM((n_cen, n_cen, 8, n), jnp.float32),
            pltpu.VMEM((n_pts, n_cen, 8, n), jnp.float32),
            pltpu.VMEM((owned, width), jnp.float32),
            pltpu.VMEM((owned, 128), jnp.float32),
            pltpu.VMEM((owned, 1), jnp.float32),
            dma((n_pts * n_cen,)),
            dma((n_pts * n_cen, 2)),
            dma((n_cen,)),
            dma((n_pts,)),
            dma((n_z,)),
            dma((n_z,)),
            dma((n_z, n_cen)),
            dma((n_z, 2, n_cen)),
            dma((n_z, n_cen)),
            dma((n_z, n_cen)),
            dma((n_cen,)),
            dma((n_pts,)),
            dma,
        ],
        compiler_params=pltpu.CompilerParams(
            collective_id=0, has_side_effects=True, vmem_limit_bytes=60 * 1024 * 1024
        ),
    )(codes, centroids)
    return (fresh[None], penalty.reshape(n))


def solution(mesh):
    placed = (P(("pts", "cen"), None), P(), P(), P(), P("cen", None, None))
    return jax.shard_map(
        functools.partial(body, mesh.shape["pts"], mesh.shape["cen"]),
        mesh=mesh,
        in_specs=placed,
        out_specs=(P("cen", "pts", None), P(("pts", "cen"))),
        check_vma=False,
    )
```

```python
import functools

import jax
import jax.numpy as jnp
from jax import lax
from jax.experimental import pallas as pl
from jax.experimental.pallas import tpu as pltpu
from jax.sharding import PartitionSpec as P

smoothing_scale = 16.0
MESH = pl.DeviceIdType.MESH
NT = (((1,), (1,)), ((), ()))


def encode(states, first_weight, first_bias, second_weight):
    pre = jnp.dot(states, first_weight, preferred_element_type=jnp.float32) + first_bias
    hidden = jax.nn.gelu(pre).astype(jnp.bfloat16)
    return jnp.dot(hidden, second_weight, preferred_element_type=jnp.float32).astype(jnp.bfloat16)


def scaled_squares(rows):
    wide = rows.astype(jnp.float32)
    return jnp.sum(wide * wide, axis=1, keepdims=True) / smoothing_scale


def kernel(
    n_pts, n_cen, codes_ref, cen_ref, out_ref, pen_ref,
    allc, stat, norm, weighted, counts, own_sq,
    recv, half, stat_recv, norm_recv,
    send_up, send_down, send_x, send_c, send_core, send_hx, send_hc, send_stat, send_norm, own_sem,
):
    n, width = codes_ref.shape
    n_z = n_pts // 4
    p, c = lax.axis_index("pts"), lax.axis_index("cen")
    core, x, z = lax.rem(p, 2), lax.rem(p // 2, 2), p // 4

    def pts_of(zi, xi, ki):
        return (zi * 2 + xi) * 2 + ki

    def z_at(k):
        return lax.rem(z + k, n_z)

    def c_at(j):
        return lax.rem(c + j, n_cen)

    def block(zi, xi, ki, ci):
        return pts_of(zi, xi, ki) * n_cen + ci

    x_peer = (pts_of(z, 1 - x, core), c)
    core_peer = (pts_of(z, x, 1 - core), c)
    mine = block(z, x, core, c)

    def remote(src, dst, send_sem, recv_sem, peer):
        return pltpu.make_async_remote_copy(
            src_ref=src, dst_ref=dst, send_sem=send_sem, recv_sem=recv_sem,
            device_id=peer, device_id_type=MESH,
        )

    def push(copy):
        copy.start()

    def whole(b, send_sem, peer, src=None):
        push(remote(allc.at[b] if src is None else src, allc.at[b], send_sem, recv.at[b], peer))

    def part(b, h, send_sem, peer):
        rows = pl.ds(h * (n // 2), n // 2)
        push(remote(allc.at[b, rows], allc.at[b, rows], send_sem, half.at[b, h], peer))

    def arrived(b):
        remote(allc.at[b], allc.at[b], own_sem, recv.at[b], core_peer).wait_recv()

    def part_arrived(b, h):
        rows = pl.ds(h * (n // 2), n // 2)
        remote(allc.at[b, rows], allc.at[b, rows], own_sem, half.at[b, h], core_peer).wait_recv()

    has_up, has_down = z < n_z - 1, z > 0
    up_peer = (pts_of(lax.rem(z + 1, n_z), x, core), c)
    down_peer = (pts_of(lax.rem(z + n_z - 1, n_z), x, core), c)

    def at_distance(d, visit):
        if d == 0:
            visit(z)
            return

        @pl.when(z + d < n_z)
        def _():
            visit(z + d)

        @pl.when(z >= d)
        def _():
            visit(z - d)

    def fan_out(zi, src=None):
        b = block(zi, x, core, c)

        @pl.when(jnp.logical_and(has_up, zi <= z))
        def _():
            whole(b, send_up.at[zi], up_peer, src)

        @pl.when(jnp.logical_and(has_down, zi >= z))
        def _():
            whole(b, send_down.at[zi], down_peer, src)

        for j in range(1, n_cen):
            whole(b, send_c.at[zi, j], (p, c_at(j)), src)
        whole(b, send_x.at[zi], x_peer, src)
        whole(b, send_core.at[zi, 0, 0], core_peer, src)

    def from_line(zi):
        arrived(block(zi, x, core, c))
        fan_out(zi)

    def from_cen(zi):
        for j in range(1, n_cen):
            b = block(zi, x, core, c_at(j))
            arrived(b)
            part(b, 1, send_hx.at[zi, j], x_peer)
            whole(b, send_core.at[zi, 0, j], core_peer)

    def from_x(zi):
        b = block(zi, 1 - x, core, c)
        arrived(b)
        for j in range(1, n_cen):
            part(b, 0, send_hc.at[zi, j], (p, c_at(j)))
        whole(b, send_core.at[zi, 1, 0], core_peer)

    def from_both(zi):
        for j in range(1, n_cen):
            b = block(zi, 1 - x, core, c_at(j))
            part_arrived(b, 0)
            part_arrived(b, 1)
            whole(b, send_core.at[zi, 1, j], core_peer)

    barrier = pltpu.get_barrier_semaphore()
    for k in range(1, n_pts):
        pl.semaphore_signal(
            barrier, inc=1, device_id=(lax.rem(p + k, n_pts), c), device_id_type=MESH
        )
    for j in range(1, n_cen):
        pl.semaphore_signal(barrier, inc=1, device_id=(p, c_at(j)), device_id_type=MESH)
    pl.semaphore_wait(barrier, n_pts - 1 + n_cen - 1)

    own = pltpu.make_async_copy(codes_ref, allc.at[mine], own_sem)
    own.start()
    fan_out(z, codes_ref)
    own.wait()

    owned = out_ref.shape[0]
    own_rows = pl.ds(pl.multiple_of(p * owned, owned), owned)
    own_sq[...] = scaled_squares(cen_ref[0, own_rows, :])

    from_cen(z)

    tile = min(256, cen_ref.shape[1])
    group_rows = n * n_cen
    group = pl.ds(p * n_cen, n_cen)

    def stats_step(i, carry):
        peak, total = carry
        centers = cen_ref[0, pl.ds(pl.multiple_of(i * tile, tile), tile), :]
        rows = allc[group].reshape(group_rows, width)
        scores = lax.dot_general(centers, rows, NT, preferred_element_type=jnp.float32)
        scores = scores * (2.0 / smoothing_scale) - scaled_squares(centers)
        peak_next = jnp.maximum(peak, jnp.max(scores, axis=0, keepdims=True))
        total_next = total * jnp.exp(peak - peak_next) + jnp.sum(
            jnp.exp(scores - peak_next), axis=0, keepdims=True
        )
        return peak_next, total_next

    tiles = cen_ref.shape[1] // tile
    stats = (
        jnp.full((1, group_rows), -jnp.inf, jnp.float32),
        jnp.zeros((1, group_rows), jnp.float32),
    )
    for d in range(1, n_z + 1):
        lo, hi = tiles * (d - 1) // n_z, tiles * d // n_z
        stats = lax.fori_loop(lo, hi, stats_step, stats)
        if d < n_z:
            at_distance(d, from_line)
            at_distance(d - 1, from_x)
            if d > 1:
                at_distance(d - 1, from_cen)
    peak, total = stats
    first = lax.broadcasted_iota(jnp.int32, (8, n), 0) == 0
    for j in range(n_cen):
        cols = slice(j * n, (j + 1) * n)
        stat[c, j] = jnp.where(first, peak[:, cols], total[:, cols])
    for j in range(1, n_cen):
        push(remote(stat.at[c], stat.at[c], send_stat.at[j], stat_recv.at[c], (p, c_at(j))))
    at_distance(n_z - 1, from_x)
    if n_z > 1:
        at_distance(n_z - 1, from_cen)

    for j in range(1, n_cen):
        s = c_at(j)
        remote(stat.at[s], stat.at[s], own_sem, stat_recv.at[s], (p, s)).wait_recv()
    for j in range(n_cen):
        top = stat[0, j][0:1, :]
        for s in range(1, n_cen):
            top = jnp.maximum(top, stat[s, j][0:1, :])
        mass = jnp.zeros_like(top)
        for s in range(n_cen):
            piece = stat[s, j]
            mass = mass + piece[1:2, :] * jnp.exp(piece[0:1, :] - top)
        norm[p, :, j * n:(j + 1) * n] = jnp.broadcast_to(top + jnp.log(mass), (8, n))
    for k in range(1, n_pts):
        push(
            remote(
                norm.at[p], norm.at[p], send_norm.at[k], norm_recv.at[p],
                (lax.rem(p + k, n_pts), c),
            )
        )
    wide = codes_ref[...].astype(jnp.float32)
    lengths = lax.dot_general(
        jnp.ones((8, width), jnp.float32), wide * wide, NT,
        preferred_element_type=jnp.float32, precision=lax.Precision.HIGHEST,
    )
    pen_ref[...] = (-(smoothing_scale / width)) * (
        norm[p, 0:1, pl.ds(pl.multiple_of(c * n, n), n)] - lengths[0:1, :] / smoothing_scale
    )

    for k in range(1, n_pts):
        s = lax.rem(p + k, n_pts)
        remote(norm.at[s], norm.at[s], own_sem, norm_recv.at[s], (s, c)).wait_recv()

    weighted[...] = jnp.zeros_like(weighted)
    counts[...] = jnp.zeros_like(counts)

    def consume(pi):
        rows = allc[pl.ds(pi * n_cen, n_cen)].reshape(group_rows, width)
        scores = lax.dot_general(
            cen_ref[0, own_rows, :], rows, NT, preferred_element_type=jnp.float32
        )
        resp = jnp.exp(scores * (2.0 / smoothing_scale) - own_sq[...] - norm[pi, 0:1, :])
        lanes = resp[:, 0:128]
        for q in range(1, group_rows // 128):
            lanes = lanes + resp[:, q * 128:(q + 1) * 128]
        counts[...] += lanes
        weighted[...] += jnp.dot(
            resp.astype(jnp.bfloat16), rows, preferred_element_type=jnp.float32
        )

    def line(i, _):
        from_both(z_at(i))
        consume(pts_of(z_at(i), x, core))
        return 0

    def across(i, _):
        consume(pts_of(z_at(i), 1 - x, core))
        return 0

    def other_core(i, _):
        zi, xi = z_at(lax.rem(i, n_z)), lax.rem(x + i // n_z, 2)
        for ci in range(n_cen):
            arrived(block(zi, xi, 1 - core, ci))
        consume(pts_of(zi, xi, 1 - core))
        return 0

    lax.fori_loop(0, n_z, line, 0)
    lax.fori_loop(0, n_z, across, 0)
    lax.fori_loop(0, 2 * n_z, other_core, 0)

    tally = jnp.sum(counts[...], axis=1, keepdims=True)
    out_ref[...] = (weighted[...] + cen_ref[0, own_rows, :].astype(jnp.float32)) / (tally + 1.0)

    def left(ref, send_sem):
        remote(ref, ref, send_sem, own_sem, core_peer).wait_send()

    block_ref, half_ref = allc.at[0], allc.at[0, pl.ds(0, n // 2)]
    for zi in range(n_z):

        @pl.when(jnp.logical_and(has_up, zi <= z))
        def _():
            left(block_ref, send_up.at[zi])

        @pl.when(jnp.logical_and(has_down, zi >= z))
        def _():
            left(block_ref, send_down.at[zi])

        left(block_ref, send_x.at[zi])
        for j in range(n_cen):
            left(block_ref, send_core.at[zi, 0, j])
            left(block_ref, send_core.at[zi, 1, j])
            if j > 0:
                left(block_ref, send_c.at[zi, j])
                left(half_ref, send_hx.at[zi, j])
                left(half_ref, send_hc.at[zi, j])
    for j in range(1, n_cen):
        left(stat.at[0], send_stat.at[j])
    for k in range(1, n_pts):
        left(norm.at[0], send_norm.at[k])


def finish(fresh_ref, pen_ref, out_ref, cost_ref):
    out_ref[0] = fresh_ref[...]
    cost_ref[...] = pen_ref[0]


def body(n_pts, n_cen, states, first_weight, first_bias, second_weight, centroids):
    codes = encode(states, first_weight, first_bias, second_weight)
    n, width = codes.shape
    owned = centroids.shape[1] // n_pts
    n_z = n_pts // 4
    dma = pltpu.SemaphoreType.DMA
    fresh, penalty = pl.pallas_call(
        functools.partial(kernel, n_pts, n_cen),
        out_shape=(
            jax.ShapeDtypeStruct((owned, width), jnp.float32),
            jax.ShapeDtypeStruct((1, n), jnp.float32),
        ),
        in_specs=[pl.BlockSpec(memory_space=pltpu.VMEM)] * 2,
        out_specs=(pl.BlockSpec(memory_space=pltpu.VMEM),) * 2,
        scratch_shapes=[
            pltpu.VMEM((n_pts * n_cen, n, width), jnp.bfloat16),
            pltpu.VMEM((n_cen, n_cen, 8, n), jnp.float32),
            pltpu.VMEM((n_pts, 8, n_cen * n), jnp.float32),
            pltpu.VMEM((owned, width), jnp.float32),
            pltpu.VMEM((owned, 128), jnp.float32),
            pltpu.VMEM((owned, 1), jnp.float32),
            dma((n_pts * n_cen,)),
            dma((n_pts * n_cen, 2)),
            dma((n_cen,)),
            dma((n_pts,)),
            dma((n_z,)),
            dma((n_z,)),
            dma((n_z,)),
            dma((n_z, n_cen)),
            dma((n_z, 2, n_cen)),
            dma((n_z, n_cen)),
            dma((n_z, n_cen)),
            dma((n_cen,)),
            dma((n_pts,)),
            dma,
        ],
        compiler_params=pltpu.CompilerParams(
            collective_id=0, has_side_effects=True, vmem_limit_bytes=60 * 1024 * 1024
        ),
    )(codes, centroids)
    return pl.pallas_call(
        finish,
        out_shape=(
            jax.ShapeDtypeStruct((1, owned, width), jnp.float32),
            jax.ShapeDtypeStruct((n,), jnp.float32),
        ),
        in_specs=[pl.BlockSpec(memory_space=pltpu.VMEM)] * 2,
        out_specs=(pl.BlockSpec(memory_space=pltpu.VMEM),) * 2,
    )(fresh, penalty)


def solution(mesh):
    placed = (P(("pts", "cen"), None), P(), P(), P(), P("cen", None, None))
    return jax.shard_map(
        functools.partial(body, mesh.shape["pts"], mesh.shape["cen"]),
        mesh=mesh,
        in_specs=placed,
        out_specs=(P("cen", "pts", None), P(("pts", "cen"))),
        check_vma=False,
    )
```

```python
import functools

import jax
import jax.numpy as jnp
from jax import lax
from jax.experimental import pallas as pl
from jax.experimental.pallas import tpu as pltpu
from jax.sharding import PartitionSpec as P

smoothing_scale = 16.0
MESH = pl.DeviceIdType.MESH
NT = (((1,), (1,)), ((), ()))


def scaled_squares(rows):
    wide = rows.astype(jnp.float32)
    return jnp.sum(wide * wide, axis=1, keepdims=True) / smoothing_scale


def kernel(
    n_pts, n_cen, states_hbm, first_hbm, bias_ref, second_hbm, cen_hbm, out_ref, pen_ref,
    states_ref, first_ref, second_ref, cen_ref, load_sem,
    allc, stat, norm, weighted, counts, own_sq,
    recv, half, stat_recv, norm_recv,
    send_up, send_down, send_x, send_c, send_core, send_hx, send_hc, send_stat, send_norm, own_sem,
):
    n, width = states_ref.shape[0], second_ref.shape[1]
    loads = [
        pltpu.make_async_copy(src, dst, load_sem.at[i])
        for i, (src, dst) in enumerate(
            (
                (states_hbm, states_ref),
                (first_hbm, first_ref),
                (second_hbm, second_ref),
                (cen_hbm.at[0], cen_ref),
            )
        )
    ]
    for load in loads:
        load.start()
    n_z = n_pts // 4
    p, c = lax.axis_index("pts"), lax.axis_index("cen")
    core, x, z = lax.rem(p, 2), lax.rem(p // 2, 2), p // 4

    def pts_of(zi, xi, ki):
        return (zi * 2 + xi) * 2 + ki

    def z_at(k):
        return lax.rem(z + k, n_z)

    def c_at(j):
        return lax.rem(c + j, n_cen)

    def block(zi, xi, ki, ci):
        return pts_of(zi, xi, ki) * n_cen + ci

    x_peer = (pts_of(z, 1 - x, core), c)
    core_peer = (pts_of(z, x, 1 - core), c)
    mine = block(z, x, core, c)

    def remote(src, dst, send_sem, recv_sem, peer):
        return pltpu.make_async_remote_copy(
            src_ref=src, dst_ref=dst, send_sem=send_sem, recv_sem=recv_sem,
            device_id=peer, device_id_type=MESH,
        )

    def push(copy):
        copy.start()

    def whole(b, send_sem, peer):
        push(remote(allc.at[b], allc.at[b], send_sem, recv.at[b], peer))

    def part(b, h, send_sem, peer):
        rows = pl.ds(h * (n // 2), n // 2)
        push(remote(allc.at[b, rows], allc.at[b, rows], send_sem, half.at[b, h], peer))

    def arrived(b):
        remote(allc.at[b], allc.at[b], own_sem, recv.at[b], core_peer).wait_recv()

    def part_arrived(b, h):
        rows = pl.ds(h * (n // 2), n // 2)
        remote(allc.at[b, rows], allc.at[b, rows], own_sem, half.at[b, h], core_peer).wait_recv()

    has_up, has_down = z < n_z - 1, z > 0
    up_peer = (pts_of(lax.rem(z + 1, n_z), x, core), c)
    down_peer = (pts_of(lax.rem(z + n_z - 1, n_z), x, core), c)

    def at_distance(d, visit):
        if d == 0:
            visit(z)
            return

        @pl.when(z + d < n_z)
        def _():
            visit(z + d)

        @pl.when(z >= d)
        def _():
            visit(z - d)

    def fan_out(zi):
        b = block(zi, x, core, c)

        @pl.when(jnp.logical_and(has_up, zi <= z))
        def _():
            whole(b, send_up.at[zi], up_peer)

        @pl.when(jnp.logical_and(has_down, zi >= z))
        def _():
            whole(b, send_down.at[zi], down_peer)

        for j in range(1, n_cen):
            whole(b, send_c.at[zi, j], (p, c_at(j)))
        whole(b, send_x.at[zi], x_peer)
        whole(b, send_core.at[zi, 0, 0], core_peer)

    def from_line(zi):
        arrived(block(zi, x, core, c))
        fan_out(zi)

    def from_cen(zi):
        for j in range(1, n_cen):
            b = block(zi, x, core, c_at(j))
            arrived(b)
            part(b, 1, send_hx.at[zi, j], x_peer)
            whole(b, send_core.at[zi, 0, j], core_peer)

    def from_x(zi):
        b = block(zi, 1 - x, core, c)
        arrived(b)
        for j in range(1, n_cen):
            part(b, 0, send_hc.at[zi, j], (p, c_at(j)))
        whole(b, send_core.at[zi, 1, 0], core_peer)

    def from_both(zi):
        for j in range(1, n_cen):
            b = block(zi, 1 - x, core, c_at(j))
            part_arrived(b, 0)
            part_arrived(b, 1)
            whole(b, send_core.at[zi, 1, j], core_peer)

    barrier = pltpu.get_barrier_semaphore()
    for k in range(1, n_pts):
        pl.semaphore_signal(
            barrier, inc=1, device_id=(lax.rem(p + k, n_pts), c), device_id_type=MESH
        )
    for j in range(1, n_cen):
        pl.semaphore_signal(barrier, inc=1, device_id=(p, c_at(j)), device_id_type=MESH)
    loads[0].wait()
    loads[1].wait()
    pre = jnp.dot(states_ref[...], first_ref[...], preferred_element_type=jnp.float32)
    hidden = jax.nn.gelu(pre + bias_ref[...][None, :]).astype(jnp.bfloat16)
    loads[2].wait()
    allc[mine] = jnp.dot(
        hidden, second_ref[...], preferred_element_type=jnp.float32
    ).astype(jnp.bfloat16)
    loads[3].wait()
    owned = out_ref.shape[0]
    own_rows = pl.ds(pl.multiple_of(p * owned, owned), owned)
    own_sq[...] = scaled_squares(cen_ref[own_rows, :])
    pl.semaphore_wait(barrier, n_pts - 1 + n_cen - 1)
    fan_out(z)

    from_cen(z)

    tile = min(512, cen_ref.shape[0])
    group_rows = n * n_cen
    group = pl.ds(p * n_cen, n_cen)

    def stats_step(i, carry):
        peak, total = carry
        centers = cen_ref[pl.ds(pl.multiple_of(i * tile, tile), tile), :]
        rows = allc[group].reshape(group_rows, width)
        scores = lax.dot_general(centers, rows, NT, preferred_element_type=jnp.float32)
        scores = scores * (2.0 / smoothing_scale) - scaled_squares(centers)
        peak_next = jnp.maximum(peak, jnp.max(scores, axis=0, keepdims=True))
        total_next = total * jnp.exp(peak - peak_next) + jnp.sum(
            jnp.exp(scores - peak_next), axis=0, keepdims=True
        )
        return peak_next, total_next

    tiles = cen_ref.shape[0] // tile
    stats = (
        jnp.full((1, group_rows), -jnp.inf, jnp.float32),
        jnp.zeros((1, group_rows), jnp.float32),
    )
    for d in range(1, n_z + 1):
        lo, hi = tiles * (d - 1) // n_z, tiles * d // n_z
        stats = lax.fori_loop(lo, hi, stats_step, stats)
        if d < n_z:
            at_distance(d, from_line)
            at_distance(d - 1, from_x)
            if d > 1:
                at_distance(d - 1, from_cen)
    peak, total = stats
    first = lax.broadcasted_iota(jnp.int32, (8, n), 0) == 0
    for j in range(n_cen):
        cols = slice(j * n, (j + 1) * n)
        stat[c, j] = jnp.where(first, peak[:, cols], total[:, cols])
    for j in range(1, n_cen):
        push(remote(stat.at[c], stat.at[c], send_stat.at[j], stat_recv.at[c], (p, c_at(j))))
    at_distance(n_z - 1, from_x)
    if n_z > 1:
        at_distance(n_z - 1, from_cen)

    for j in range(1, n_cen):
        s = c_at(j)
        remote(stat.at[s], stat.at[s], own_sem, stat_recv.at[s], (p, s)).wait_recv()
    for j in range(n_cen):
        top = stat[0, j][0:1, :]
        for s in range(1, n_cen):
            top = jnp.maximum(top, stat[s, j][0:1, :])
        mass = jnp.zeros_like(top)
        for s in range(n_cen):
            piece = stat[s, j]
            mass = mass + piece[1:2, :] * jnp.exp(piece[0:1, :] - top)
        norm[p, :, j * n:(j + 1) * n] = jnp.broadcast_to(top + jnp.log(mass), (8, n))
    for k in range(1, n_pts):
        push(
            remote(
                norm.at[p], norm.at[p], send_norm.at[k], norm_recv.at[p],
                (lax.rem(p + k, n_pts), c),
            )
        )
    wide = allc[mine].astype(jnp.float32)
    lengths = lax.dot_general(
        jnp.ones((8, width), jnp.float32), wide * wide, NT,
        preferred_element_type=jnp.float32, precision=lax.Precision.HIGHEST,
    )
    pen_ref[...] = (-(smoothing_scale / width)) * (
        norm[p, 0:1, pl.ds(pl.multiple_of(c * n, n), n)] - lengths[0:1, :] / smoothing_scale
    )

    for k in range(1, n_pts):
        s = lax.rem(p + k, n_pts)
        remote(norm.at[s], norm.at[s], own_sem, norm_recv.at[s], (s, c)).wait_recv()

    weighted[...] = jnp.zeros_like(weighted)
    counts[...] = jnp.zeros_like(counts)

    def consume(pi):
        rows = allc[pl.ds(pi * n_cen, n_cen)].reshape(group_rows, width)
        scores = lax.dot_general(
            cen_ref[own_rows, :], rows, NT, preferred_element_type=jnp.float32
        )
        resp = jnp.exp(scores * (2.0 / smoothing_scale) - own_sq[...] - norm[pi, 0:1, :])
        lanes = resp[:, 0:128]
        for q in range(1, group_rows // 128):
            lanes = lanes + resp[:, q * 128:(q + 1) * 128]
        counts[...] += lanes
        weighted[...] += jnp.dot(
            resp.astype(jnp.bfloat16), rows, preferred_element_type=jnp.float32
        )

    def line(i, _):
        from_both(z_at(i))
        consume(pts_of(z_at(i), x, core))
        return 0

    def across(i, _):
        consume(pts_of(z_at(i), 1 - x, core))
        return 0

    def other_core(i, _):
        zi, xi = z_at(lax.rem(i, n_z)), lax.rem(x + i // n_z, 2)
        for ci in range(n_cen):
            arrived(block(zi, xi, 1 - core, ci))
        consume(pts_of(zi, xi, 1 - core))
        return 0

    lax.fori_loop(0, n_z, line, 0, unroll=n_z <= 4)
    lax.fori_loop(0, n_z, across, 0, unroll=n_z <= 4)
    lax.fori_loop(0, 2 * n_z, other_core, 0, unroll=n_z <= 4)

    tally = jnp.sum(counts[...], axis=1, keepdims=True)
    out_ref[...] = (weighted[...] + cen_ref[own_rows, :].astype(jnp.float32)) / (tally + 1.0)

    def left(ref, send_sem):
        remote(ref, ref, send_sem, own_sem, core_peer).wait_send()

    block_ref, half_ref = allc.at[0], allc.at[0, pl.ds(0, n // 2)]
    for zi in range(n_z):

        @pl.when(jnp.logical_and(has_up, zi <= z))
        def _():
            left(block_ref, send_up.at[zi])

        @pl.when(jnp.logical_and(has_down, zi >= z))
        def _():
            left(block_ref, send_down.at[zi])

        left(block_ref, send_x.at[zi])
        for j in range(n_cen):
            left(block_ref, send_core.at[zi, 0, j])
            left(block_ref, send_core.at[zi, 1, j])
            if j > 0:
                left(block_ref, send_c.at[zi, j])
                left(half_ref, send_hx.at[zi, j])
                left(half_ref, send_hc.at[zi, j])
    for j in range(1, n_cen):
        left(stat.at[0], send_stat.at[j])
    for k in range(1, n_pts):
        left(norm.at[0], send_norm.at[k])


def finish(fresh_ref, pen_ref, out_ref, cost_ref):
    out_ref[0] = fresh_ref[...]
    cost_ref[...] = pen_ref[0]


def body(n_pts, n_cen, states, first_weight, first_bias, second_weight, centroids):
    n, width = states.shape[0], second_weight.shape[1]
    owned = centroids.shape[1] // n_pts
    n_z = n_pts // 4
    dma = pltpu.SemaphoreType.DMA
    fresh, penalty = pl.pallas_call(
        functools.partial(kernel, n_pts, n_cen),
        out_shape=(
            jax.ShapeDtypeStruct((owned, width), jnp.float32),
            jax.ShapeDtypeStruct((1, n), jnp.float32),
        ),
        in_specs=[
            pl.BlockSpec(memory_space=pl.ANY),
            pl.BlockSpec(memory_space=pl.ANY),
            pl.BlockSpec(memory_space=pltpu.VMEM),
            pl.BlockSpec(memory_space=pl.ANY),
            pl.BlockSpec(memory_space=pl.ANY),
        ],
        out_specs=(pl.BlockSpec(memory_space=pltpu.VMEM),) * 2,
        scratch_shapes=[
            pltpu.VMEM(states.shape, states.dtype),
            pltpu.VMEM(first_weight.shape, first_weight.dtype),
            pltpu.VMEM(second_weight.shape, second_weight.dtype),
            pltpu.VMEM(centroids.shape[1:], centroids.dtype),
            dma((4,)),
            pltpu.VMEM((n_pts * n_cen, n, width), jnp.bfloat16),
            pltpu.VMEM((n_cen, n_cen, 8, n), jnp.float32),
            pltpu.VMEM((n_pts, 8, n_cen * n), jnp.float32),
            pltpu.VMEM((owned, width), jnp.float32),
            pltpu.VMEM((owned, 128), jnp.float32),
            pltpu.VMEM((owned, 1), jnp.float32),
            dma((n_pts * n_cen,)),
            dma((n_pts * n_cen, 2)),
            dma((n_cen,)),
            dma((n_pts,)),
            dma((n_z,)),
            dma((n_z,)),
            dma((n_z,)),
            dma((n_z, n_cen)),
            dma((n_z, 2, n_cen)),
            dma((n_z, n_cen)),
            dma((n_z, n_cen)),
            dma((n_cen,)),
            dma((n_pts,)),
            dma,
        ],
        compiler_params=pltpu.CompilerParams(
            collective_id=0, has_side_effects=True, vmem_limit_bytes=60 * 1024 * 1024
        ),
    )(states, first_weight, first_bias, second_weight, centroids)
    return pl.pallas_call(
        finish,
        out_shape=(
            jax.ShapeDtypeStruct((1, owned, width), jnp.float32),
            jax.ShapeDtypeStruct((n,), jnp.float32),
        ),
        in_specs=[pl.BlockSpec(memory_space=pltpu.VMEM)] * 2,
        out_specs=(pl.BlockSpec(memory_space=pltpu.VMEM),) * 2,
    )(fresh, penalty)


def solution(mesh):
    placed = (P(("pts", "cen"), None), P(), P(), P(), P("cen", None, None))
    return jax.shard_map(
        functools.partial(body, mesh.shape["pts"], mesh.shape["cen"]),
        mesh=mesh,
        in_specs=placed,
        out_specs=(P("cen", "pts", None), P(("pts", "cen"))),
        check_vma=False,
    )
```
